32 devices in a mesh: dp: 8 (over y, x, core), fsdp: 4 (over z).
Axes of the slice: x: 2, y: 2, z: 4, core: 2. Of those that a mesh axis runs over, the one named last changes fastest.
Arguments:
- acts: bfloat16 [16384, 8192], P(('dp', 'fsdp')), may hold values from -6 to 6
- grad_out: bfloat16 [16384, 1024], P(('dp', 'fsdp')), may hold values from -6 to 6
- codes: int32 [128, 16, 1024], P('fsdp'), may hold values from 0 to 65535
- scale_codes: int32 [128, 1024], P('fsdp'), may hold values from 0 to 255
- col_scale: float32 [1024], replicated, may hold values from 0.03 to 0.3
- down_adapter: bfloat16 [64, 8192], P(None, 'fsdp'), may hold values from -0.1796875 to 0.1796875
- up_adapter: bfloat16 [64, 1024], P(None, 'fsdp'), may hold values from -0.1875 to 0.1875
Outputs:
- input_gradient: bfloat16 [16384, 8192], P(('dp', 'fsdp'))
- grad_down: float32 [64, 8192], P(None, 'fsdp')
- grad_up: float32 [64, 1024], P(None, 'fsdp')
The draws below stay inside these ranges and needn't reach their ends.
All inputs are finite; a program needn't handle non-finite values.
Results may differ from the reference program's by a relative error of at most 0.0059.
Values may be sent and summed in bfloat16 or wider, within the bound.
A program may use at most 128 MiB of HBM per device.

```python
import math
import jax
import jax.numpy as jnp
from jax import lax

D = 8192
O = 1024
R = 64
TOK_DEV = 512
TOKEN_TOTAL = 16384


def touch_ends(array, own_key, smallest, top_value):
    longest = array.shape.index(max(array.shape))
    spots = []
    for shift in (0, 1):
        where = [jax.random.randint(jax.random.fold_in(own_key, axis), (), 0, length) for axis, length in enumerate(array.shape)]
        where[longest] = (where[longest] + shift) % array.shape[longest]
        spots.append(tuple(where))
    return array.at[spots[0]].set(smallest).at[spots[1]].set(top_value)


def strengthened(result, key, source, target, blocks, factor):
    def block_of(dim):
        return (jnp.arange(result.shape[dim]) // (result.shape[dim] // blocks)).reshape((-1,) + (1,) * (result.ndim - 1 - dim))

    first = jax.random.permutation(key, blocks)[block_of(target)]
    far = (block_of(target) + blocks // 2) % blocks
    return jnp.where((block_of(source) == first) | (block_of(source) == far), factor * result, result)


def block_levels(key, shape, cuts, smallest, largest):
    def one(dim, shards_of):
        steps = jax.random.uniform(jax.random.fold_in(jax.random.fold_in(key, 6), dim), (shards_of,), jnp.float32, smallest / len(cuts), largest / len(cuts))
        return jnp.repeat(jnp.exp(steps), shape[dim] // shards_of).reshape((-1,) + (1,) * (len(shape) - dim - 1))

    level = one(*cuts[0])
    for cut in cuts[1:]:
        level = level * one(*cut)
    return level


def bell_draw(stream_key, extent, width, bound, cuts=(), kind=jnp.bfloat16):
    result = width * jax.random.normal(stream_key, extent, jnp.float32)
    if cuts:
        result = result * block_levels(stream_key, extent, cuts, -0.22, 0.18)
    return jnp.clip(result, -bound, bound).astype(kind)


def gaussian_with(stream_key, shape, deviation, limit, pieces, heavy, dtype=jnp.bfloat16):
    drawn = deviation * jax.random.normal(stream_key, shape, jnp.float32)
    if pieces:
        drawn = drawn * block_levels(stream_key, shape, pieces, -0.22, 0.18)
    return jnp.clip(strengthened(drawn, jax.random.fold_in(stream_key, 3), *heavy), -limit, limit).astype(dtype)


def setup_inputs(seed: int = 0) -> dict:
    arg_keys = jax.random.split(jax.random.key(seed), 8)
    acts = gaussian_with(arg_keys[0], (TOKEN_TOTAL, D), 1.0, 6.0, ((0, 32),), (0, 1, 32, 2.75))
    grad_out = gaussian_with(arg_keys[1], (TOKEN_TOTAL, O), 1.0, 6.0, ((0, 32),), (0, 1, 32, 2.75))
    codes = touch_ends(jax.random.randint(arg_keys[2], (D // 64, 16, O), 0, 65536), jax.random.fold_in(arg_keys[2], 1), 0, 65535).astype(jnp.int32)
    scale_codes = touch_ends(jax.random.randint(arg_keys[3], (D // 64, O), 0, 256), jax.random.fold_in(arg_keys[3], 1), 0, 255).astype(jnp.int32)
    col_scale = jnp.clip(jnp.exp(jax.random.uniform(arg_keys[4], (O,), jnp.float32, math.log(0.03), math.log(0.3))), 0.03, 0.3)
    down_adapter = bell_draw(arg_keys[5], (R, D), 0.03, 0.1796875, ((1, 4),))
    up_adapter = bell_draw(arg_keys[6], (R, O), O ** -0.5, 0.1875, ((1, 4),))
    return {"acts": acts, "grad_out": grad_out, "codes": codes, "scale_codes": scale_codes, "col_scale": col_scale, "down_adapter": down_adapter, "up_adapter": up_adapter}


adapter_scale = 0.5
nf4_table = [-1.0, -0.6961928009986877, -0.5250730514526367, -0.39491748809814453, -0.28444138169288635, -0.18477343022823334, -0.09105003625154495, 0.0, 0.07958029955625534, 0.16093020141124725, 0.24611230194568634, 0.33791524171829224, 0.44070982933044434, 0.5626170039176941, 0.7229568362236023, 1.0]


def dequantize(codes, scale_codes, col_scale):
    block_count = codes.shape[0]
    columns = codes.shape[2]
    nibbles = jnp.stack([(codes >> (4 * nibble_pos)) & 15 for nibble_pos in range(4)], axis=2)
    levels = jnp.zeros(nibbles.shape, jnp.float32)
    for position, quantum in enumerate(nf4_table):
        levels = jnp.where(nibbles == position, jnp.float32(quantum), levels)
    absmax = (scale_codes.astype(jnp.float32) + 1.0) / 256.0 * col_scale[None, :]
    weight = levels * absmax[:, None, None, :]
    return weight.reshape(block_count * 64, columns).astype(jnp.bfloat16)


def reference(acts, grad_out, codes, scale_codes, col_scale, down_adapter, up_adapter):
    weight = dequantize(codes, scale_codes, col_scale)
    blocks_in = acts.reshape(TOKEN_TOTAL // TOK_DEV, TOK_DEV, D)
    blocks_out = grad_out.reshape(TOKEN_TOTAL // TOK_DEV, TOK_DEV, O)
    scale_factor = adapter_scale * TOKEN_TOTAL ** -0.5

    def one_block(carry, pair):
        act_rows, grad_rows = pair
        mixed = jnp.dot(grad_rows, up_adapter.T, preferred_element_type=jnp.float32).astype(jnp.bfloat16)
        lowered = jnp.dot(act_rows, down_adapter.T, preferred_element_type=jnp.float32).astype(jnp.bfloat16)
        frozen_base = lax.dot_general(grad_rows, weight, (((1,), (1,)), ((), ())), preferred_element_type=jnp.float32)
        operand_side = jnp.dot(mixed, down_adapter, preferred_element_type=jnp.float32)
        incoming_gradient_rows = (frozen_base + adapter_scale * operand_side).astype(jnp.bfloat16)
        term_down = lax.dot_general(mixed, act_rows, (((0,), (0,)), ((), ())), preferred_element_type=jnp.float32)
        term_up = lax.dot_general(lowered, grad_rows, (((0,), (0,)), ((), ())), preferred_element_type=jnp.float32)
        return (carry[0] + term_down, carry[1] + term_up), incoming_gradient_rows

    start = (jnp.zeros((R, D), jnp.float32), jnp.zeros((R, O), jnp.float32))
    totals, grad_blocks = lax.scan(one_block, start, (blocks_in, blocks_out))
    input_gradient = grad_blocks.reshape(TOKEN_TOTAL, D)
    return input_gradient, scale_factor * totals[0], scale_factor * totals[1]
```

```python
import functools

import jax
import jax.numpy as jnp
from jax import lax
from jax.experimental import pallas as pl
from jax.experimental.pallas import tpu as pltpu
from jax.sharding import PartitionSpec as P

MESH = pl.DeviceIdType.MESH
NT = (((1,), (1,)), ((), ()))
adapter_scale = 0.5
nf4_table = [
    -1.0,
    -0.6961928009986877,
    -0.5250730514526367,
    -0.39491748809814453,
    -0.28444138169288635,
    -0.18477343022823334,
    -0.09105003625154495,
    0.0,
    0.07958029955625534,
    0.16093020141124725,
    0.24611230194568634,
    0.33791524171829224,
    0.44070982933044434,
    0.5626170039176941,
    0.7229568362236023,
    1.0,
]
GROUP = 8


def levels_of(words, nibble):
    rows = [jnp.float32(v) for v in nf4_table]
    for bit in range(4):
        on = (words & (1 << (4 * nibble + bit))) != 0
        rows = [jnp.where(on, rows[2 * i + 1], rows[2 * i]) for i in range(len(rows) // 2)]
    return rows[0]


def kernel(Z, DP, factor, acts_hbm, grad_hbm, codes_hbm, scale_ref, col_ref, down_hbm, up_hbm,
           out_hbm, gdown_ref, gup_ref,
           acts, grad, codes, weight, downf, upf, stage, outb, mix, terms,
           g1s, g1r, g2s, g2r, g3r, fin,
           load_sem, down_sem, out_sem, send_sem, w_sem, d_sem, u_sem, g1_sem, g2_sem, g3_sem, g4_sem):
    d, z = lax.axis_index("dp"), lax.axis_index("fsdp")
    p, core = lax.rem(d, GROUP), lax.rem(d, 2)
    xbit, ybit = lax.rem(d // 2, 2), lax.rem(d // 4, 2)
    dx, dy, ds_ = 2 - 4 * xbit, 4 - 8 * ybit, 1 - 2 * core
    half_rows, width = weight.shape[3], weight.shape[4]
    tile = 2 * half_rows
    shard = GROUP * tile
    R = mix.shape[1]
    RH = R // 2
    up_width = upf.shape[2]
    half_blocks = half_rows // 64

    def source(k):
        m = jnp.minimum(z, Z - 1 - z)
        paired = jnp.where(k % 2 == 0, z - (k // 2 + 1), z + (k // 2 + 1))
        rest = jnp.where(2 * z < Z - 1, z + (k - m + 1), z - (k - m + 1))
        return jnp.where(k < 2 * m, paired, rest)

    at_x, at_y, at_s, at_d = (d + dx, z), (d + dy, z), (d + ds_, z), (d + dx + dy, z)
    pairs = DP // 2
    others = [lax.rem(d + 2 * j, DP) for j in range(1, pairs)]

    loads = [
        pltpu.make_async_copy(codes_hbm, codes, load_sem.at[0]),
        pltpu.make_async_copy(up_hbm, upf.at[z], load_sem.at[1]),
        pltpu.make_async_copy(grad_hbm, grad, load_sem.at[2]),
        pltpu.make_async_copy(acts_hbm, acts, load_sem.at[3]),
    ]
    down_loads = [
        pltpu.make_async_copy(down_hbm.at[:, q * tile:(q + 1) * tile], downf.at[z, q], down_sem.at[q])
        for q in range(GROUP)
    ]
    loads[0].start()
    loads[1].start()
    for c in down_loads:
        c.start()
    loads[2].start()
    loads[3].start()

    barrier = pltpu.get_barrier_semaphore()
    for k in range(Z - 1):
        pl.semaphore_signal(barrier, inc=1, device_id=(d, source(k)), device_id_type=MESH)
    for o in others:
        pl.semaphore_signal(barrier, inc=1, device_id=(o, z), device_id_type=MESH)
    pl.semaphore_signal(barrier, inc=1, device_id=at_s, device_id_type=MESH)

    sends = []

    def send(src, dst, sem, to):
        c = pltpu.make_async_remote_copy(src_ref=src, dst_ref=dst, send_sem=send_sem.at[len(sends)],
                                         recv_sem=sem, device_id=to, device_id_type=MESH)
        c.start()
        sends.append(c)

    def arrived(ref, sem):
        pltpu.make_async_remote_copy(src_ref=ref, dst_ref=ref, send_sem=send_sem.at[0], recv_sem=sem,
                                     device_id=at_s, device_id_type=MESH).wait_recv()

    def send_w(s, h, q, to):
        send(weight.at[s, h, q], weight.at[s, h, q], w_sem.at[s, h, q], to)

    def wait_w(s, h, q):
        arrived(weight.at[s, h, q], w_sem.at[s, h, q])

    def send_d(s, q, to):
        send(downf.at[s, q], downf.at[s, q], d_sem.at[s, q], to)

    def wait_d(s, q):
        arrived(downf.at[s, q], d_sem.at[s, q])

    def dequantize(h, q):
        for r in range(half_blocks):
            b = (h * GROUP + q) * half_blocks + r

            def columns(c, _, b=b, r=r):
                cols = pl.ds(pl.multiple_of(c * 256, 256), 256)
                words = codes[b, :, cols]
                absmax = (scale_ref[pl.ds(b, 1), cols].astype(jnp.float32) + 1.0) / 256.0 * col_ref[:, cols]
                for j in range(4):
                    stage[pl.ds(j, 16, stride=4), :] = levels_of(words, j)[:, :128] * absmax[:, :128]
                    stage[pl.ds(64 + j, 16, stride=4), :] = levels_of(words, j)[:, 128:] * absmax[:, 128:]
                weight[z, h, q, pl.ds(r * 64, 64), pl.ds(pl.multiple_of(c * 256, 128), 128)] = stage[0:64].astype(jnp.bfloat16)
                weight[z, h, q, pl.ds(r * 64, 64), pl.ds(pl.multiple_of(c * 256 + 128, 128), 128)] = stage[64:128].astype(jnp.bfloat16)
                return 0

            lax.fori_loop(0, width // 256, columns, 0)

    def tiles(s, h):
        def one(t, _):
            rows = weight[s, h, pl.ds(2 * t, 2)].reshape(tile, width)
            tt = h * 4 + t
            acc = lax.dot_general(grad[...], rows, NT, preferred_element_type=jnp.float32)
            acc += adapter_scale * jnp.dot(mix[...], downf[s, tt], preferred_element_type=jnp.float32)
            slot = s * GROUP + tt
            outb[slot] = acc.astype(jnp.bfloat16)
            pltpu.make_async_copy(outb.at[slot], out_hbm.at[:, pl.ds(pl.multiple_of(slot * tile, tile), tile)],
                                  out_sem.at[slot]).start()
            return 0

        lax.fori_loop(0, 4, one, 0)

    px, py, ps = p + dx, p + dy, p + ds_
    pd = p + dx + dy
    same_core = (p, px, py, pd)
    events = 2 * (Z - 1)

    def service(i):
        if 0 <= i < events:
            s, h = source(i // 2), i % 2
            wait_w(s, h, p)
            send_w(s, h, p, at_x)
            send_w(s, h, p, at_y)
            send_w(s, h, p, at_s)
        if 0 <= i - 1 < events:
            s, h = source((i - 1) // 2), (i - 1) % 2
            wait_w(s, h, px)
            if h == 0:
                send_w(s, h, px, at_y)
            send_w(s, h, px, at_s)
            wait_w(s, h, py)
            if h == 1:
                send_w(s, h, py, at_x)
            send_w(s, h, py, at_s)
        if 0 <= i - 2 < events:
            s, h = source((i - 2) // 2), (i - 2) % 2
            wait_w(s, h, pd)
            send_w(s, h, pd, at_s)
        if 0 <= i - 3 < events:
            s, h = source((i - 3) // 2), (i - 3) % 2
            for q in same_core:
                wait_w(s, h, q + ds_)
            tiles(s, h)

    def own(h):
        def one(j, _):
            dequantize(h, lax.rem(p + j, GROUP))
            return 0

        lax.fori_loop(1, GROUP, one, 0)
        tiles(z, h)

    loads[0].wait()
    dequantize(0, p)
    pl.semaphore_wait(barrier, (Z - 1) + (pairs - 1) + 1)
    loads[1].wait()
    for k in range(Z - 1):
        send(upf.at[z], upf.at[z], u_sem.at[z], (d, source(k)))
    for c in down_loads:
        c.wait()
    for k in range(Z - 1):
        send_d(z, p, (d, source(k)))
    for k in range(Z - 1):
        if k == 0:
            send_w(z, 0, p, (d, source(k)))
            dequantize(1, p)
        else:
            send_w(z, 0, p, (d, source(k)))
        send_w(z, 1, p, (d, source(k)))

    loads[2].wait()
    for k in range(Z - 1):
        arrived(upf.at[source(k)], u_sem.at[source(k)])
    mixed = jnp.zeros(mix.shape, jnp.float32)
    for s in range(Z):
        mixed += lax.dot_general(grad[:, s * up_width:(s + 1) * up_width], upf[s], NT,
                                 preferred_element_type=jnp.float32)
    mix[...] = mixed.astype(jnp.bfloat16)

    def down_first():
        for k in range(Z - 1):
            s = source(k)
            wait_d(s, p)
            for to in (at_x, at_y, at_d, at_s):
                send_d(s, p, to)

    def down_second():
        for k in range(Z - 1):
            s = source(k)
            for q in (px, py, pd):
                wait_d(s, q)
                send_d(s, q, at_s)

    def down_third():
        for k in range(Z - 1):
            for q in same_core:
                wait_d(source(k), q + ds_)

    def gradient_terms():
        loads[3].wait()
        mixed_t = mix[...].astype(jnp.float32).T.astype(jnp.bfloat16)

        def one(t, low):
            s, q = t // GROUP, lax.rem(t, GROUP)
            a = acts[:, pl.ds(pl.multiple_of(t * tile, tile), tile)]
            terms[s, :, pl.ds(pl.multiple_of(q * tile, tile), tile)] = jnp.dot(
                mixed_t, a, preferred_element_type=jnp.float32)
            return low + lax.dot_general(a, downf[s, q], NT, preferred_element_type=jnp.float32)

        low = lax.fori_loop(0, Z * GROUP, one, jnp.zeros(mix.shape, jnp.float32))
        low_t = low.astype(jnp.bfloat16).astype(jnp.float32).T.astype(jnp.bfloat16)
        for s in range(Z):
            terms[s, :, shard:shard + up_width] = jnp.dot(
                low_t, grad[:, s * up_width:(s + 1) * up_width], preferred_element_type=jnp.float32)
        mine, theirs = pl.multiple_of(core * RH, RH), pl.multiple_of((1 - core) * RH, RH)
        for s in range(Z):
            g1s[s] = terms[s, pl.ds(theirs, RH), :].astype(jnp.bfloat16)
        send(g1s, g1r, g1_sem.at[0], at_s)

    def reduce_core():
        arrived(g1r, g1_sem.at[0])
        mine = pl.multiple_of(core * RH, RH)
        for s in range(Z):
            total = terms[s, pl.ds(mine, RH), :] + g1r[s].astype(jnp.float32)
            terms[s, pl.ds(mine, RH), :] = total
            g2s[s] = total.astype(jnp.bfloat16)
        for k in range(Z - 1):
            s = source(k)
            send(g2s.at[s], g2r.at[z], g2_sem.at[z], (d, s))

    def reduce_fsdp():
        mine = pl.multiple_of(core * RH, RH)
        total = terms[z, pl.ds(mine, RH), :]
        for k in range(Z - 1):
            s = source(k)
            arrived(g2r.at[s], g2_sem.at[s])
            total += g2r[s].astype(jnp.float32)
        slot = d // 2
        g3r[slot] = total.astype(jnp.bfloat16)
        for o in others:
            send(g3r.at[slot], g3r.at[slot], g3_sem.at[slot], (o, z))

    def reduce_dp():
        for o in others:
            arrived(g3r.at[o // 2], g3_sem.at[o // 2])
        total = g3r[0].astype(jnp.float32)
        for j in range(1, pairs):
            total += g3r[j].astype(jnp.float32)
        fin[core] = factor * total
        send(fin.at[core], fin.at[core], g4_sem.at[0], at_s)

    def finish():
        arrived(fin.at[1 - core], g4_sem.at[0])
        for c in range(2):
            gdown_ref[c * RH:(c + 1) * RH, :] = fin[c, :, :shard]
            gup_ref[c * RH:(c + 1) * RH, :] = fin[c, :, shard:shard + up_width]

    work = [
        lambda: (down_first(), own(0)),
        lambda: (down_second(), own(1)),
        lambda: (down_third(), gradient_terms()),
        reduce_core,
        reduce_fsdp,
        reduce_dp,
        finish,
    ]
    for i in range(events + 3):
        service(i)
        if i < len(work):
            work[i]()
    for c in sends:
        c.wait_send()

    def drain(t, _):
        pltpu.make_async_copy(outb.at[t], out_hbm.at[:, pl.ds(pl.multiple_of(t * tile, tile), tile)],
                              out_sem.at[t]).wait()
        return 0

    lax.fori_loop(0, Z * GROUP, drain, 0)


def solution(mesh):
    Z, DP = mesh.shape["fsdp"], mesh.shape["dp"]
    bf16, f32 = jnp.bfloat16, jnp.float32

    def local(acts, grad_out, codes, scale_codes, col_scale, down_adapter, up_adapter):
        tokens, D = acts.shape
        O = grad_out.shape[1]
        R, shard = down_adapter.shape
        up_width = up_adapter.shape[1]
        tile = shard // GROUP
        wide = shard + up_width
        RH = R // 2
        factor = adapter_scale * float(tokens * Z * DP) ** (-0.5)
        n_sends = (Z - 1) * (1 + 1 + 2 + 2 * 8 + 4 + 3 + 1) + 1 + (DP // 2 - 1) + 1
        DMA = pltpu.SemaphoreType.DMA
        anywhere, vmem = pl.BlockSpec(memory_space=pl.ANY), pl.BlockSpec(memory_space=pltpu.VMEM)
        return pl.pallas_call(
            functools.partial(kernel, Z, DP, factor),
            out_shape=(
                jax.ShapeDtypeStruct((tokens, D), bf16),
                jax.ShapeDtypeStruct((R, shard), f32),
                jax.ShapeDtypeStruct((R, up_width), f32),
            ),
            in_specs=[anywhere, anywhere, anywhere, vmem, vmem, anywhere, anywhere],
            out_specs=(anywhere, vmem, vmem),
            scratch_shapes=[
                pltpu.VMEM((tokens, D), bf16),
                pltpu.VMEM((tokens, O), bf16),
                pltpu.VMEM(codes.shape, jnp.int32),
                pltpu.VMEM((Z, 2, GROUP, tile // 2, O), bf16),
                pltpu.VMEM((Z, GROUP, R, tile), bf16),
                pltpu.VMEM((Z, R, up_width), bf16),
                pltpu.VMEM((128, 128), f32),
                pltpu.VMEM((Z * GROUP, tokens, tile), bf16),
                pltpu.VMEM((tokens, R), bf16),
                pltpu.VMEM((Z, R, wide), f32),
                pltpu.VMEM((Z, RH, wide), bf16),
                pltpu.VMEM((Z, RH, wide), bf16),
                pltpu.VMEM((Z, RH, wide), bf16),
                pltpu.VMEM((Z, RH, wide), bf16),
                pltpu.VMEM((DP // 2, RH, wide), bf16),
                pltpu.VMEM((2, RH, wide), f32),
                DMA((4,)), DMA((GROUP,)), DMA((Z * GROUP,)), DMA((n_sends,)),
                DMA((Z, 2, GROUP)), DMA((Z, GROUP)), DMA((Z,)),
                DMA((1,)), DMA((Z,)), DMA((DP // 2,)), DMA((1,)),
            ],
            compiler_params=pltpu.CompilerParams(
                collective_id=0, has_side_effects=True, vmem_limit_bytes=60 * 1024 * 1024
            ),
        )(acts, grad_out, codes, scale_codes, col_scale.reshape(1, -1), down_adapter, up_adapter)

    placed = (
        P(("dp", "fsdp"), None),
        P(("dp", "fsdp"), None),
        P("fsdp", None, None),
        P("fsdp", None),
        P(),
        P(None, "fsdp"),
        P(None, "fsdp"),
    )
    return jax.shard_map(
        local,
        mesh=mesh,
        in_specs=placed,
        out_specs=(P(("dp", "fsdp"), None), P(None, "fsdp"), P(None, "fsdp")),
        check_vma=False,
    )
```

```python
import functools

import jax
import jax.numpy as jnp
from jax import lax
from jax.experimental import pallas as pl
from jax.experimental.pallas import tpu as pltpu
from jax.sharding import PartitionSpec as P

MESH = pl.DeviceIdType.MESH
NT = (((1,), (1,)), ((), ()))
adapter_scale = 0.5
nf4_table = [
    -1.0,
    -0.6961928009986877,
    -0.5250730514526367,
    -0.39491748809814453,
    -0.28444138169288635,
    -0.18477343022823334,
    -0.09105003625154495,
    0.0,
    0.07958029955625534,
    0.16093020141124725,
    0.24611230194568634,
    0.33791524171829224,
    0.44070982933044434,
    0.5626170039176941,
    0.7229568362236023,
    1.0,
]
GROUP = 8


def levels_of(words, nibble):
    rows = [jnp.float32(v) for v in nf4_table]
    for bit in range(4):
        on = (words & (1 << (4 * nibble + bit))) != 0
        rows = [jnp.where(on, rows[2 * i + 1], rows[2 * i]) for i in range(len(rows) // 2)]
    return rows[0]


def kernel(Z, DP, factor, acts_hbm, grad_hbm, codes_hbm, scale_ref, col_ref, down_hbm, up_hbm,
           out_hbm, gdown_ref, gup_ref,
           acts, grad, codes, weight, downf, upf, stage, outb, mix, terms,
           g1s, g1r, g2s, g2r, g3r, fin,
           load_sem, down_sem, out_sem, send_sem, w_sem, d_sem, u_sem, g1_sem, g2_sem, g3_sem, g4_sem):
    d, z = lax.axis_index("dp"), lax.axis_index("fsdp")
    p, core = lax.rem(d, GROUP), lax.rem(d, 2)
    xbit, ybit = lax.rem(d // 2, 2), lax.rem(d // 4, 2)
    dx, dy, ds_ = 2 - 4 * xbit, 4 - 8 * ybit, 1 - 2 * core
    half_rows, width = weight.shape[3], weight.shape[4]
    tile = 2 * half_rows
    shard = GROUP * tile
    R = mix.shape[1]
    RH = R // 2
    up_width = upf.shape[2]
    half_blocks = half_rows // 64

    def source(k):
        m = jnp.minimum(z, Z - 1 - z)
        paired = jnp.where(k % 2 == 0, z - (k // 2 + 1), z + (k // 2 + 1))
        rest = jnp.where(2 * z < Z - 1, z + (k - m + 1), z - (k - m + 1))
        return jnp.where(k < 2 * m, paired, rest)

    at_x, at_y, at_s, at_d = (d + dx, z), (d + dy, z), (d + ds_, z), (d + dx + dy, z)
    pairs = DP // 2
    others = [lax.rem(d + 2 * j, DP) for j in range(1, pairs)]

    loads = [
        pltpu.make_async_copy(codes_hbm, codes, load_sem.at[0]),
        pltpu.make_async_copy(up_hbm, upf.at[z], load_sem.at[1]),
        pltpu.make_async_copy(grad_hbm, grad, load_sem.at[2]),
        pltpu.make_async_copy(acts_hbm, acts, load_sem.at[3]),
    ]
    down_loads = [
        pltpu.make_async_copy(down_hbm.at[:, q * tile:(q + 1) * tile], downf.at[z, q], down_sem.at[q])
        for q in range(GROUP)
    ]
    loads[0].start()
    loads[1].start()
    for c in down_loads:
        c.start()
    loads[2].start()
    loads[3].start()

    barrier = pltpu.get_barrier_semaphore()
    for k in range(Z - 1):
        pl.semaphore_signal(barrier, inc=1, device_id=(d, source(k)), device_id_type=MESH)
    for o in others:
        pl.semaphore_signal(barrier, inc=1, device_id=(o, z), device_id_type=MESH)
    pl.semaphore_signal(barrier, inc=1, device_id=at_s, device_id_type=MESH)

    sends, conditions = [], {}

    def send(src, dst, sem, to):
        c = pltpu.make_async_remote_copy(src_ref=src, dst_ref=dst, send_sem=send_sem.at[len(sends)],
                                         recv_sem=sem, device_id=to, device_id_type=MESH)
        c.start()
        sends.append(c)

    def send_if(on, src, dst, sem, to):
        c = pltpu.make_async_remote_copy(src_ref=src, dst_ref=dst, send_sem=send_sem.at[len(sends)],
                                         recv_sem=sem, device_id=to, device_id_type=MESH)
        pl.when(on)(c.start)
        sends.append(c)
        conditions[len(sends) - 1] = on

    def arrived(ref, sem):
        pltpu.make_async_remote_copy(src_ref=ref, dst_ref=ref, send_sem=send_sem.at[0], recv_sem=sem,
                                     device_id=at_s, device_id_type=MESH).wait_recv()

    def send_w(s, h, q, to):
        send(weight.at[s, h, q], weight.at[s, h, q], w_sem.at[s, h, q], to)

    def wait_w(s, h, q):
        arrived(weight.at[s, h, q], w_sem.at[s, h, q])

    def send_d(s, q, to):
        send(downf.at[s, q], downf.at[s, q], d_sem.at[s, q], to)

    def wait_d(s, q):
        arrived(downf.at[s, q], d_sem.at[s, q])

    def dequantize(h, q):
        for r in range(half_blocks):
            b = (h * GROUP + q) * half_blocks + r

            def columns(c, _, b=b, r=r):
                cols = pl.ds(pl.multiple_of(c * 256, 256), 256)
                words = codes[b, :, cols]
                absmax = (scale_ref[pl.ds(b, 1), cols].astype(jnp.float32) + 1.0) / 256.0 * col_ref[:, cols]
                for j in range(4):
                    stage[pl.ds(j, 16, stride=4), :] = levels_of(words, j)[:, :128] * absmax[:, :128]
                    stage[pl.ds(64 + j, 16, stride=4), :] = levels_of(words, j)[:, 128:] * absmax[:, 128:]
                weight[z, h, q, pl.ds(r * 64, 64), pl.ds(pl.multiple_of(c * 256, 128), 128)] = stage[0:64].astype(jnp.bfloat16)
                weight[z, h, q, pl.ds(r * 64, 64), pl.ds(pl.multiple_of(c * 256 + 128, 128), 128)] = stage[64:128].astype(jnp.bfloat16)
                return 0

            lax.fori_loop(0, width // 256, columns, 0)

    def tiles(s, h):
        def one(t, _):
            rows = weight[s, h, pl.ds(2 * t, 2)].reshape(tile, width)
            tt = h * 4 + t
            acc = lax.dot_general(grad[...], rows, NT, preferred_element_type=jnp.float32)
            acc += adapter_scale * jnp.dot(mix[...], downf[s, tt], preferred_element_type=jnp.float32)
            slot = s * GROUP + tt
            outb[slot] = acc.astype(jnp.bfloat16)
            pltpu.make_async_copy(outb.at[slot], out_hbm.at[:, pl.ds(pl.multiple_of(slot * tile, tile), tile)],
                                  out_sem.at[slot]).start()
            return 0

        lax.fori_loop(0, 4, one, 0)

    px, py, ps = p + dx, p + dy, p + ds_
    pd = p + dx + dy
    same_core = (p, px, py, pd)
    events = 2 * (Z - 1)

    def passes_on(s):
        return ((s < z) & (z < Z - 1)) | ((s > z) & (z > 0))

    def pass_on(i):
        if 0 <= i < events:
            s, h = source(i // 2), i % 2
            on = passes_on(s)
            pl.when(on)(lambda: wait_w(s, h, p))
            piece = weight.at[s, h, p]
            to = jnp.where(on, z + jnp.where(s < z, 1, -1), source(0))
            send_if(on, piece, piece, w_sem.at[s, h, p], (d, to))

    def service(i):
        if i < 2:
            pass_on(i)
        if 0 <= i < events:
            s, h = source(i // 2), i % 2
            pl.when(jnp.logical_not(passes_on(s)))(lambda: wait_w(s, h, p))
            send_w(s, h, p, at_x)
            send_w(s, h, p, at_y)
            send_w(s, h, p, at_s)
        pass_on(i + 2)
        if 0 <= i - 1 < events:
            s, h = source((i - 1) // 2), (i - 1) % 2
            wait_w(s, h, px)
            if h == 0:
                send_w(s, h, px, at_y)
            send_w(s, h, px, at_s)
            wait_w(s, h, py)
            if h == 1:
                send_w(s, h, py, at_x)
            send_w(s, h, py, at_s)
        if 0 <= i - 2 < events:
            s, h = source((i - 2) // 2), (i - 2) % 2
            wait_w(s, h, pd)
            send_w(s, h, pd, at_s)
        if 0 <= i - 3 < events:
            s, h = source((i - 3) // 2), (i - 3) % 2
            for q in same_core:
                wait_w(s, h, q + ds_)
            tiles(s, h)

    def own(h):
        def one(j, _):
            dequantize(h, lax.rem(p + j, GROUP))
            return 0

        lax.fori_loop(1, GROUP, one, 0)
        tiles(z, h)

    loads[0].wait()
    dequantize(0, p)
    pl.semaphore_wait(barrier, (Z - 1) + (pairs - 1) + 1)
    loads[1].wait()
    for k in range(Z - 1):
        send(upf.at[z], upf.at[z], u_sem.at[z], (d, source(k)))
    for c in down_loads:
        c.wait()
    for k in range(Z - 1):
        send_d(z, p, (d, source(k)))
    for h in range(2):
        piece = weight.at[z, h, p]
        for on, to in ((z < Z - 1, jnp.where(z < Z - 1, z + 1, z - 1)), (z > 0, jnp.where(z > 0, z - 1, z + 1))):
            send_if(on, piece, piece, w_sem.at[z, h, p], (d, to))
        if h == 0:
            dequantize(1, p)

    loads[2].wait()
    for k in range(Z - 1):
        arrived(upf.at[source(k)], u_sem.at[source(k)])
    mixed = jnp.zeros(mix.shape, jnp.float32)
    for s in range(Z):
        mixed += lax.dot_general(grad[:, s * up_width:(s + 1) * up_width], upf[s], NT,
                                 preferred_element_type=jnp.float32)
    mix[...] = mixed.astype(jnp.bfloat16)

    def down_first():
        for k in range(Z - 1):
            s = source(k)
            wait_d(s, p)
            for to in (at_x, at_y, at_d, at_s):
                send_d(s, p, to)

    def down_second():
        for k in range(Z - 1):
            s = source(k)
            for q in (px, py, pd):
                wait_d(s, q)
                send_d(s, q, at_s)

    def down_third():
        for k in range(Z - 1):
            for q in same_core:
                wait_d(source(k), q + ds_)

    def gradient_terms():
        loads[3].wait()
        mixed_t = mix[...].astype(jnp.float32).T.astype(jnp.bfloat16)

        def one(t, low):
            s, q = t // GROUP, lax.rem(t, GROUP)
            a = acts[:, pl.ds(pl.multiple_of(t * tile, tile), tile)]
            terms[s, :, pl.ds(pl.multiple_of(q * tile, tile), tile)] = jnp.dot(
                mixed_t, a, preferred_element_type=jnp.float32)
            return low + lax.dot_general(a, downf[s, q], NT, preferred_element_type=jnp.float32)

        low = lax.fori_loop(0, Z * GROUP, one, jnp.zeros(mix.shape, jnp.float32))
        low_t = low.astype(jnp.bfloat16).astype(jnp.float32).T.astype(jnp.bfloat16)
        for s in range(Z):
            terms[s, :, shard:shard + up_width] = jnp.dot(
                low_t, grad[:, s * up_width:(s + 1) * up_width], preferred_element_type=jnp.float32)
        mine, theirs = pl.multiple_of(core * RH, RH), pl.multiple_of((1 - core) * RH, RH)
        for s in range(Z):
            g1s[s] = terms[s, pl.ds(theirs, RH), :].astype(jnp.bfloat16)
        send(g1s, g1r, g1_sem.at[0], at_s)

    def reduce_core():
        arrived(g1r, g1_sem.at[0])
        mine = pl.multiple_of(core * RH, RH)
        for s in range(Z):
            total = terms[s, pl.ds(mine, RH), :] + g1r[s].astype(jnp.float32)
            terms[s, pl.ds(mine, RH), :] = total
            g2s[s] = total.astype(jnp.bfloat16)
        for k in range(Z - 1):
            s = source(k)
            send(g2s.at[s], g2r.at[z], g2_sem.at[z], (d, s))

    def reduce_fsdp():
        mine = pl.multiple_of(core * RH, RH)
        total = terms[z, pl.ds(mine, RH), :]
        for k in range(Z - 1):
            s = source(k)
            arrived(g2r.at[s], g2_sem.at[s])
            total += g2r[s].astype(jnp.float32)
        slot = d // 2
        g3r[slot] = total.astype(jnp.bfloat16)
        for o in others:
            send(g3r.at[slot], g3r.at[slot], g3_sem.at[slot], (o, z))

    def reduce_dp():
        for o in others:
            arrived(g3r.at[o // 2], g3_sem.at[o // 2])
        total = g3r[0].astype(jnp.float32)
        for j in range(1, pairs):
            total += g3r[j].astype(jnp.float32)
        fin[core] = factor * total
        send(fin.at[core], fin.at[core], g4_sem.at[0], at_s)

    def finish():
        arrived(fin.at[1 - core], g4_sem.at[0])
        for c in range(2):
            gdown_ref[c * RH:(c + 1) * RH, :] = fin[c, :, :shard]
            gup_ref[c * RH:(c + 1) * RH, :] = fin[c, :, shard:shard + up_width]

    work = [
        lambda: (down_first(), own(0)),
        lambda: (down_second(), own(1)),
        lambda: (down_third(), gradient_terms()),
        reduce_core,
        reduce_fsdp,
        reduce_dp,
        finish,
    ]
    for i in range(events + 3):
        service(i)
        if i < len(work):
            work[i]()
    for j, c in enumerate(sends):
        if j in conditions:
            pl.when(conditions[j])(c.wait_send)
        else:
            c.wait_send()

    def drain(t, _):
        pltpu.make_async_copy(outb.at[t], out_hbm.at[:, pl.ds(pl.multiple_of(t * tile, tile), tile)],
                              out_sem.at[t]).wait()
        return 0

    lax.fori_loop(0, Z * GROUP, drain, 0)


def solution(mesh):
    Z, DP = mesh.shape["fsdp"], mesh.shape["dp"]
    bf16, f32 = jnp.bfloat16, jnp.float32

    def local(acts, grad_out, codes, scale_codes, col_scale, down_adapter, up_adapter):
        tokens, D = acts.shape
        O = grad_out.shape[1]
        R, shard = down_adapter.shape
        up_width = up_adapter.shape[1]
        tile = shard // GROUP
        wide = shard + up_width
        RH = R // 2
        factor = adapter_scale * float(tokens * Z * DP) ** (-0.5)
        n_sends = 4 + (Z - 1) * (1 + 1 + 2 * 9 + 4 + 3 + 1) + 1 + (DP // 2 - 1) + 1
        DMA = pltpu.SemaphoreType.DMA
        anywhere, vmem = pl.BlockSpec(memory_space=pl.ANY), pl.BlockSpec(memory_space=pltpu.VMEM)
        return pl.pallas_call(
            functools.partial(kernel, Z, DP, factor),
            out_shape=(
                jax.ShapeDtypeStruct((tokens, D), bf16),
                jax.ShapeDtypeStruct((R, shard), f32),
                jax.ShapeDtypeStruct((R, up_width), f32),
            ),
            in_specs=[anywhere, anywhere, anywhere, vmem, vmem, anywhere, anywhere],
            out_specs=(anywhere, vmem, vmem),
            scratch_shapes=[
                pltpu.VMEM((tokens, D), bf16),
                pltpu.VMEM((tokens, O), bf16),
                pltpu.VMEM(codes.shape, jnp.int32),
                pltpu.VMEM((Z, 2, GROUP, tile // 2, O), bf16),
                pltpu.VMEM((Z, GROUP, R, tile), bf16),
                pltpu.VMEM((Z, R, up_width), bf16),
                pltpu.VMEM((128, 128), f32),
                pltpu.VMEM((Z * GROUP, tokens, tile), bf16),
                pltpu.VMEM((tokens, R), bf16),
                pltpu.VMEM((Z, R, wide), f32),
                pltpu.VMEM((Z, RH, wide), bf16),
                pltpu.VMEM((Z, RH, wide), bf16),
                pltpu.VMEM((Z, RH, wide), bf16),
                pltpu.VMEM((Z, RH, wide), bf16),
                pltpu.VMEM((DP // 2, RH, wide), bf16),
                pltpu.VMEM((2, RH, wide), f32),
                DMA((4,)), DMA((GROUP,)), DMA((Z * GROUP,)), DMA((n_sends,)),
                DMA((Z, 2, GROUP)), DMA((Z, GROUP)), DMA((Z,)),
                DMA((1,)), DMA((Z,)), DMA((DP // 2,)), DMA((1,)),
            ],
            compiler_params=pltpu.CompilerParams(
                collective_id=0, has_side_effects=True, vmem_limit_bytes=60 * 1024 * 1024
            ),
        )(acts, grad_out, codes, scale_codes, col_scale.reshape(1, -1), down_adapter, up_adapter)

    placed = (
        P(("dp", "fsdp"), None),
        P(("dp", "fsdp"), None),
        P("fsdp", None, None),
        P("fsdp", None),
        P(),
        P(None, "fsdp"),
        P(None, "fsdp"),
    )
    return jax.shard_map(
        local,
        mesh=mesh,
        in_specs=placed,
        out_specs=(P(("dp", "fsdp"), None), P(None, "fsdp"), P(None, "fsdp")),
        check_vma=False,
    )
```

```python
import functools

import jax
import jax.numpy as jnp
from jax import lax
from jax.experimental import pallas as pl
from jax.experimental.pallas import tpu as pltpu
from jax.sharding import PartitionSpec as P

MESH = pl.DeviceIdType.MESH
NT = (((1,), (1,)), ((), ()))
adapter_scale = 0.5
nf4_table = [
    -1.0,
    -0.6961928009986877,
    -0.5250730514526367,
    -0.39491748809814453,
    -0.28444138169288635,
    -0.18477343022823334,
    -0.09105003625154495,
    0.0,
    0.07958029955625534,
    0.16093020141124725,
    0.24611230194568634,
    0.33791524171829224,
    0.44070982933044434,
    0.5626170039176941,
    0.7229568362236023,
    1.0,
]
GROUP = 8


def levels_of(words, nibble):
    rows = [jnp.float32(v) for v in nf4_table]
    for bit in range(4):
        on = (words & (1 << (4 * nibble + bit))) != 0
        rows = [jnp.where(on, rows[2 * i + 1], rows[2 * i]) for i in range(len(rows) // 2)]
    return rows[0]


def kernel(Z, DP, factor, acts_hbm, grad_hbm, codes_hbm, scale_ref, col_ref, down_hbm, up_hbm,
           out_hbm, gdown_ref, gup_ref,
           acts, grad, codes, weight, downf, upf, stage, outb, mix, terms,
           g1s, g1r, g2s, g2r, g3r, fin,
           load_sem, down_sem, out_sem, send_sem, w_sem, d_sem, u_sem, g1_sem, g2_sem, g3_sem, g4_sem):
    d, z = lax.axis_index("dp"), lax.axis_index("fsdp")
    p, core = lax.rem(d, GROUP), lax.rem(d, 2)
    xbit, ybit = lax.rem(d // 2, 2), lax.rem(d // 4, 2)
    dx, dy, ds_ = 2 - 4 * xbit, 4 - 8 * ybit, 1 - 2 * core
    half_rows, width = weight.shape[3], weight.shape[4]
    tile = 2 * half_rows
    shard = GROUP * tile
    R = mix.shape[1]
    RH = R // 2
    up_width = upf.shape[2]
    half_blocks = half_rows // 64

    def source(k):
        m = jnp.minimum(z, Z - 1 - z)
        paired = jnp.where(k % 2 == 0, z - (k // 2 + 1), z + (k // 2 + 1))
        rest = jnp.where(2 * z < Z - 1, z + (k - m + 1), z - (k - m + 1))
        return jnp.where(k < 2 * m, paired, rest)

    at_x, at_y, at_s, at_d = (d + dx, z), (d + dy, z), (d + ds_, z), (d + dx + dy, z)
    pairs = DP // 2
    others = [lax.rem(d + 2 * j, DP) for j in range(1, pairs)]

    loads = [
        pltpu.make_async_copy(codes_hbm, codes, load_sem.at[0]),
        pltpu.make_async_copy(up_hbm, upf.at[z], load_sem.at[1]),
        pltpu.make_async_copy(grad_hbm, grad, load_sem.at[2]),
        pltpu.make_async_copy(acts_hbm, acts, load_sem.at[3]),
    ]
    down_loads = [
        pltpu.make_async_copy(down_hbm.at[:, q * tile:(q + 1) * tile], downf.at[z, q], down_sem.at[q])
        for q in range(GROUP)
    ]
    loads[0].start()
    loads[1].start()
    for c in down_loads:
        c.start()
    loads[2].start()
    loads[3].start()

    barrier = pltpu.get_barrier_semaphore()
    for k in range(Z - 1):
        pl.semaphore_signal(barrier, inc=1, device_id=(d, source(k)), device_id_type=MESH)
    for o in others:
        pl.semaphore_signal(barrier, inc=1, device_id=(o, z), device_id_type=MESH)
    pl.semaphore_signal(barrier, inc=1, device_id=at_s, device_id_type=MESH)

    sends, conditions = [], {}

    def send(src, dst, sem, to):
        c = pltpu.make_async_remote_copy(src_ref=src, dst_ref=dst, send_sem=send_sem.at[len(sends)],
                                         recv_sem=sem, device_id=to, device_id_type=MESH)
        c.start()
        sends.append(c)

    def send_if(on, src, dst, sem, to):
        c = pltpu.make_async_remote_copy(src_ref=src, dst_ref=dst, send_sem=send_sem.at[len(sends)],
                                         recv_sem=sem, device_id=to, device_id_type=MESH)
        pl.when(on)(c.start)
        sends.append(c)
        conditions[len(sends) - 1] = on

    def arrived(ref, sem):
        pltpu.make_async_remote_copy(src_ref=ref, dst_ref=ref, send_sem=send_sem.at[0], recv_sem=sem,
                                     device_id=at_s, device_id_type=MESH).wait_recv()

    def send_w(s, h, q, to):
        send(weight.at[s, h, q], weight.at[s, h, q], w_sem.at[s, h, q], to)

    def wait_w(s, h, q):
        arrived(weight.at[s, h, q], w_sem.at[s, h, q])

    def send_d(s, q, to):
        send(downf.at[s, q], downf.at[s, q], d_sem.at[s, q], to)

    def wait_d(s, q):
        arrived(downf.at[s, q], d_sem.at[s, q])

    def dequantize(h, q):
        for r in range(half_blocks):
            b = (h * GROUP + q) * half_blocks + r

            def columns(c, _, b=b, r=r):
                cols = pl.ds(pl.multiple_of(c * 256, 256), 256)
                words = codes[b, :, cols]
                absmax = (scale_ref[pl.ds(b, 1), cols].astype(jnp.float32) + 1.0) / 256.0 * col_ref[:, cols]
                for j in range(4):
                    stage[pl.ds(j, 16, stride=4), :] = levels_of(words, j)[:, :128] * absmax[:, :128]
                    stage[pl.ds(64 + j, 16, stride=4), :] = levels_of(words, j)[:, 128:] * absmax[:, 128:]
                weight[z, h, q, pl.ds(r * 64, 64), pl.ds(pl.multiple_of(c * 256, 128), 128)] = stage[0:64].astype(jnp.bfloat16)
                weight[z, h, q, pl.ds(r * 64, 64), pl.ds(pl.multiple_of(c * 256 + 128, 128), 128)] = stage[64:128].astype(jnp.bfloat16)
                return 0

            lax.fori_loop(0, width // 256, columns, 0)

    def tiles(s, h):
        def one(t, _):
            rows = weight[s, h, pl.ds(2 * t, 2)].reshape(tile, width)
            tt = h * 4 + t
            acc = lax.dot_general(grad[...], rows, NT, preferred_element_type=jnp.float32)
            acc += adapter_scale * jnp.dot(mix[...], downf[s, tt], preferred_element_type=jnp.float32)
            slot = s * GROUP + tt
            outb[slot] = acc.astype(jnp.bfloat16)
            pltpu.make_async_copy(outb.at[slot], out_hbm.at[:, pl.ds(pl.multiple_of(slot * tile, tile), tile)],
                                  out_sem.at[slot]).start()
            return 0

        lax.fori_loop(0, 4, one, 0)

    px, py, ps = p + dx, p + dy, p + ds_
    pd = p + dx + dy
    same_core = (p, px, py, pd)
    events = 2 * (Z - 1)

    def passes_on(s):
        return ((s < z) & (z < Z - 1)) | ((s > z) & (z > 0))

    def pass_on(i):
        if 0 <= i < events:
            s, h = source(i // 2), i % 2
            on = passes_on(s)
            pl.when(on)(lambda: wait_w(s, h, p))
            piece = weight.at[s, h, p]
            to = jnp.where(on, z + jnp.where(s < z, 1, -1), source(0))
            send_if(on, piece, piece, w_sem.at[s, h, p], (d, to))

    def at_end(s):
        return (s == 0) | (s == Z - 1)

    def pass_on_diagonal(i):
        for s in (0, Z - 1):
            away = z if s == 0 else Z - 1 - z
            for h in range(2):
                if not 1 <= i - 1 - h <= Z - 2:
                    continue
                on = away == i - 1 - h
                piece = weight.at[s, h, pd]
                pl.when(on)(lambda s=s, h=h: wait_w(s, h, pd))
                to = jnp.where(on, z + (1 if s == 0 else -1), source(0))
                send_if(on, piece, piece, w_sem.at[s, h, pd], (d, to))

    def event(i):
        return source(i // 2), i % 2

    def first(i):
        s, h = event(i)
        pl.when(jnp.logical_not(passes_on(s)))(lambda: wait_w(s, h, p))
        send_w(s, h, p, at_x)
        send_w(s, h, p, at_y)
        send_w(s, h, p, at_s)

    def second(i):
        s, h = event(i)
        inner = jnp.logical_not(at_end(s))
        wait_w(s, h, px)
        if h == 0:
            piece = weight.at[s, h, px]
            send_if(inner, piece, piece, w_sem.at[s, h, px], at_y)
        send_w(s, h, px, at_s)
        wait_w(s, h, py)
        if h == 1:
            piece = weight.at[s, h, py]
            send_if(inner, piece, piece, w_sem.at[s, h, py], at_x)
        send_w(s, h, py, at_s)

    def third(i):
        s, h = event(i)
        pl.when(jnp.logical_not(at_end(s) & passes_on(s)))(lambda: wait_w(s, h, pd))
        send_w(s, h, pd, at_s)

    def use(i):
        s, h = event(i)
        for q in same_core:
            wait_w(s, h, q + ds_)
        tiles(s, h)

    def service(i):
        if i < 2:
            pass_on(i)
        first(i)
        pass_on(i + 2)
        pass_on_diagonal(i)
        for step, back in ((second, 1), (third, 2), (use, 3)):
            if i >= back:
                step(i - back)

    def own(h):
        def one(j, _):
            m = jnp.where(j == GROUP - 3, GROUP - 1, j + 1)
            dequantize(h, p + lax.rem(m, 2) * ds_ + lax.rem(m // 2, 2) * dx + (m // 4) * dy)
            return 0

        lax.fori_loop(0, GROUP - 2, one, 0)
        tiles(z, h)

    loads[0].wait()
    dequantize(0, p)
    pl.semaphore_wait(barrier, (Z - 1) + (pairs - 1) + 1)
    loads[1].wait()
    for k in range(Z - 1):
        send(upf.at[z], upf.at[z], u_sem.at[z], (d, source(k)))
    for c in down_loads:
        c.wait()
    for k in range(Z - 1):
        send_d(z, p, (d, source(k)))
    for h in range(2):
        piece = weight.at[z, h, p]
        for on, to in ((z < Z - 1, jnp.where(z < Z - 1, z + 1, z - 1)), (z > 0, jnp.where(z > 0, z - 1, z + 1))):
            send_if(on, piece, piece, w_sem.at[z, h, p], (d, to))
        if h == 0:
            dequantize(1, p)
    for h in range(2):
        dequantize(h, pd)
        piece = weight.at[z, h, pd]
        send_if(at_end(z), piece, piece, w_sem.at[z, h, pd], (d, jnp.where(z == 0, z + 1, z - 1)))

    loads[2].wait()
    for k in range(Z - 1):
        arrived(upf.at[source(k)], u_sem.at[source(k)])
    mixed = jnp.zeros(mix.shape, jnp.float32)
    for s in range(Z):
        mixed += lax.dot_general(grad[:, s * up_width:(s + 1) * up_width], upf[s], NT,
                                 preferred_element_type=jnp.float32)
    mix[...] = mixed.astype(jnp.bfloat16)

    def down_first():
        for k in range(Z - 1):
            s = source(k)
            wait_d(s, p)
            for to in (at_x, at_y, at_d, at_s):
                send_d(s, p, to)

    def down_second():
        for k in range(Z - 1):
            s = source(k)
            for q in (px, py, pd):
                wait_d(s, q)
                send_d(s, q, at_s)

    def down_third():
        for k in range(Z - 1):
            for q in same_core:
                wait_d(source(k), q + ds_)

    def gradient_terms():
        loads[3].wait()
        mixed_t = mix[...].astype(jnp.float32).T.astype(jnp.bfloat16)

        def one(t, low):
            s, q = t // GROUP, lax.rem(t, GROUP)
            a = acts[:, pl.ds(pl.multiple_of(t * tile, tile), tile)]
            terms[s, :, pl.ds(pl.multiple_of(q * tile, tile), tile)] = jnp.dot(
                mixed_t, a, preferred_element_type=jnp.float32)
            return low + lax.dot_general(a, downf[s, q], NT, preferred_element_type=jnp.float32)

        low = lax.fori_loop(0, Z * GROUP, one, jnp.zeros(mix.shape, jnp.float32))
        low_t = low.astype(jnp.bfloat16).astype(jnp.float32).T.astype(jnp.bfloat16)
        for s in range(Z):
            terms[s, :, shard:shard + up_width] = jnp.dot(
                low_t, grad[:, s * up_width:(s + 1) * up_width], preferred_element_type=jnp.float32)
        mine, theirs = pl.multiple_of(core * RH, RH), pl.multiple_of((1 - core) * RH, RH)
        for s in range(Z):
            g1s[s] = terms[s, pl.ds(theirs, RH), :].astype(jnp.bfloat16)
        send(g1s, g1r, g1_sem.at[0], at_s)

    def reduce_core():
        arrived(g1r, g1_sem.at[0])
        mine = pl.multiple_of(core * RH, RH)
        for s in range(Z):
            total = terms[s, pl.ds(mine, RH), :] + g1r[s].astype(jnp.float32)
            terms[s, pl.ds(mine, RH), :] = total
            g2s[s] = total.astype(jnp.bfloat16)
        for k in range(Z - 1):
            s = source(k)
            send(g2s.at[s], g2r.at[z], g2_sem.at[z], (d, s))

    def reduce_fsdp():
        mine = pl.multiple_of(core * RH, RH)
        total = terms[z, pl.ds(mine, RH), :]
        for k in range(Z - 1):
            s = source(k)
            arrived(g2r.at[s], g2_sem.at[s])
            total += g2r[s].astype(jnp.float32)
        slot = d // 2
        g3r[slot] = total.astype(jnp.bfloat16)
        for o in others:
            send(g3r.at[slot], g3r.at[slot], g3_sem.at[slot], (o, z))

    def reduce_dp():
        for o in others:
            arrived(g3r.at[o // 2], g3_sem.at[o // 2])
        total = g3r[0].astype(jnp.float32)
        for j in range(1, pairs):
            total += g3r[j].astype(jnp.float32)
        fin[core] = factor * total
        send(fin.at[core], fin.at[core], g4_sem.at[0], at_s)

    def finish():
        arrived(fin.at[1 - core], g4_sem.at[0])
        for c in range(2):
            gdown_ref[c * RH:(c + 1) * RH, :] = fin[c, :, :shard]
            gup_ref[c * RH:(c + 1) * RH, :] = fin[c, :, shard:shard + up_width]

    work = [
        lambda: (down_first(), own(0)),
        lambda: (down_second(), own(1)),
        lambda: (down_third(), gradient_terms()),
        reduce_core,
        reduce_fsdp,
        reduce_dp,
        finish,
    ]
    for i in range(events):
        service(i)
        if i < len(work):
            work[i]()
    use(events - 3)
    third(events - 2)
    use(events - 2)
    for step in work[events:]:
        step()
    second(events - 1)
    third(events - 1)
    use(events - 1)
    for j, c in enumerate(sends):
        if j in conditions:
            pl.when(conditions[j])(c.wait_send)
        else:
            c.wait_send()

    def drain(t, _):
        pltpu.make_async_copy(outb.at[t], out_hbm.at[:, pl.ds(pl.multiple_of(t * tile, tile), tile)],
                              out_sem.at[t]).wait()
        return 0

    lax.fori_loop(0, Z * GROUP, drain, 0)


def solution(mesh):
    Z, DP = mesh.shape["fsdp"], mesh.shape["dp"]
    bf16, f32 = jnp.bfloat16, jnp.float32

    def local(acts, grad_out, codes, scale_codes, col_scale, down_adapter, up_adapter):
        tokens, D = acts.shape
        O = grad_out.shape[1]
        R, shard = down_adapter.shape
        up_width = up_adapter.shape[1]
        tile = shard // GROUP
        wide = shard + up_width
        RH = R // 2
        factor = adapter_scale * float(tokens * Z * DP) ** (-0.5)
        n_sends = 6 + 4 * (Z - 2) + (Z - 1) * (1 + 1 + 2 * 9 + 4 + 3 + 1) + 1 + (DP // 2 - 1) + 1
        DMA = pltpu.SemaphoreType.DMA
        anywhere, vmem = pl.BlockSpec(memory_space=pl.ANY), pl.BlockSpec(memory_space=pltpu.VMEM)
        return pl.pallas_call(
            functools.partial(kernel, Z, DP, factor),
            out_shape=(
                jax.ShapeDtypeStruct((tokens, D), bf16),
                jax.ShapeDtypeStruct((R, shard), f32),
                jax.ShapeDtypeStruct((R, up_width), f32),
            ),
            in_specs=[anywhere, anywhere, anywhere, vmem, vmem, anywhere, anywhere],
            out_specs=(anywhere, vmem, vmem),
            scratch_shapes=[
                pltpu.VMEM((tokens, D), bf16),
                pltpu.VMEM((tokens, O), bf16),
                pltpu.VMEM(codes.shape, jnp.int32),
                pltpu.VMEM((Z, 2, GROUP, tile // 2, O), bf16),
                pltpu.VMEM((Z, GROUP, R, tile), bf16),
                pltpu.VMEM((Z, R, up_width), bf16),
                pltpu.VMEM((128, 128), f32),
                pltpu.VMEM((Z * GROUP, tokens, tile), bf16),
                pltpu.VMEM((tokens, R), bf16),
                pltpu.VMEM((Z, R, wide), f32),
                pltpu.VMEM((Z, RH, wide), bf16),
                pltpu.VMEM((Z, RH, wide), bf16),
                pltpu.VMEM((Z, RH, wide), bf16),
                pltpu.VMEM((Z, RH, wide), bf16),
                pltpu.VMEM((DP // 2, RH, wide), bf16),
                pltpu.VMEM((2, RH, wide), f32),
                DMA((4,)), DMA((GROUP,)), DMA((Z * GROUP,)), DMA((n_sends,)),
                DMA((Z, 2, GROUP)), DMA((Z, GROUP)), DMA((Z,)),
                DMA((1,)), DMA((Z,)), DMA((DP // 2,)), DMA((1,)),
            ],
            compiler_params=pltpu.CompilerParams(
                collective_id=0, has_side_effects=True, vmem_limit_bytes=60 * 1024 * 1024
            ),
        )(acts, grad_out, codes, scale_codes, col_scale.reshape(1, -1), down_adapter, up_adapter)

    placed = (
        P(("dp", "fsdp"), None),
        P(("dp", "fsdp"), None),
        P("fsdp", None, None),
        P("fsdp", None),
        P(),
        P(None, "fsdp"),
        P(None, "fsdp"),
    )
    return jax.shard_map(
        local,
        mesh=mesh,
        in_specs=placed,
        out_specs=(P(("dp", "fsdp"), None), P(None, "fsdp"), P(None, "fsdp")),
        check_vma=False,
    )
```

```python
import functools

import jax
import jax.numpy as jnp
from jax import lax
from jax.experimental import pallas as pl
from jax.experimental.pallas import tpu as pltpu
from jax.sharding import PartitionSpec as P

MESH = pl.DeviceIdType.MESH
NT = (((1,), (1,)), ((), ()))
adapter_scale = 0.5
nf4_table = [
    -1.0,
    -0.6961928009986877,
    -0.5250730514526367,
    -0.39491748809814453,
    -0.28444138169288635,
    -0.18477343022823334,
    -0.09105003625154495,
    0.0,
    0.07958029955625534,
    0.16093020141124725,
    0.24611230194568634,
    0.33791524171829224,
    0.44070982933044434,
    0.5626170039176941,
    0.7229568362236023,
    1.0,
]
GROUP = 8


def levels_of(words, nibble):
    rows = [jnp.float32(v) for v in nf4_table]
    for bit in range(4):
        on = (words & (1 << (4 * nibble + bit))) != 0
        rows = [jnp.where(on, rows[2 * i + 1], rows[2 * i]) for i in range(len(rows) // 2)]
    return rows[0]


def kernel(Z, DP, factor, acts_hbm, grad_hbm, codes_hbm, scale_ref, col_ref, down_hbm, up_hbm,
           out_hbm, gdown_ref, gup_ref,
           acts, grad, codes, weight, downf, upf, stage, outb, mix, terms,
           g1s, g1r, g2s, g2r, g3r, fin,
           load_sem, down_sem, out_sem, send_sem, w_sem, d_sem, u_sem, g1_sem, g2_sem, g3_sem, g4_sem):
    d, z = lax.axis_index("dp"), lax.axis_index("fsdp")
    p, core = lax.rem(d, GROUP), lax.rem(d, 2)
    xbit, ybit = lax.rem(d // 2, 2), lax.rem(d // 4, 2)
    dx, dy, ds_ = 2 - 4 * xbit, 4 - 8 * ybit, 1 - 2 * core
    half_rows, width = weight.shape[3], weight.shape[4]
    tile = 2 * half_rows
    shard = GROUP * tile
    R = mix.shape[1]
    RH = R // 2
    up_width = upf.shape[2]
    half_blocks = half_rows // 64

    def source(k):
        m = jnp.minimum(z, Z - 1 - z)
        paired = jnp.where(k % 2 == 0, z - (k // 2 + 1), z + (k // 2 + 1))
        rest = jnp.where(2 * z < Z - 1, z + (k - m + 1), z - (k - m + 1))
        return jnp.where(k < 2 * m, paired, rest)

    at_x, at_y, at_s, at_d = (d + dx, z), (d + dy, z), (d + ds_, z), (d + dx + dy, z)
    pairs = DP // 2
    others = [lax.rem(d + 2 * j, DP) for j in range(1, pairs)]

    loads = [
        pltpu.make_async_copy(codes_hbm, codes, load_sem.at[0]),
        pltpu.make_async_copy(up_hbm, upf.at[z], load_sem.at[1]),
        pltpu.make_async_copy(grad_hbm, grad, load_sem.at[2]),
        pltpu.make_async_copy(acts_hbm, acts, load_sem.at[3]),
    ]
    down_loads = [
        pltpu.make_async_copy(down_hbm.at[:, q * tile:(q + 1) * tile], downf.at[z, q], down_sem.at[q])
        for q in range(GROUP)
    ]
    loads[0].start()
    loads[1].start()
    for c in down_loads:
        c.start()
    loads[2].start()
    loads[3].start()

    barrier = pltpu.get_barrier_semaphore()
    for k in range(Z - 1):
        pl.semaphore_signal(barrier, inc=1, device_id=(d, source(k)), device_id_type=MESH)
    for o in others:
        pl.semaphore_signal(barrier, inc=1, device_id=(o, z), device_id_type=MESH)
    pl.semaphore_signal(barrier, inc=1, device_id=at_s, device_id_type=MESH)

    sends, conditions = [], {}

    def send(src, dst, sem, to):
        c = pltpu.make_async_remote_copy(src_ref=src, dst_ref=dst, send_sem=send_sem.at[len(sends)],
                                         recv_sem=sem, device_id=to, device_id_type=MESH)
        c.start()
        sends.append(c)

    def send_if(on, src, dst, sem, to):
        c = pltpu.make_async_remote_copy(src_ref=src, dst_ref=dst, send_sem=send_sem.at[len(sends)],
                                         recv_sem=sem, device_id=to, device_id_type=MESH)
        pl.when(on)(c.start)
        sends.append(c)
        conditions[len(sends) - 1] = on

    def arrived(ref, sem):
        pltpu.make_async_remote_copy(src_ref=ref, dst_ref=ref, send_sem=send_sem.at[0], recv_sem=sem,
                                     device_id=at_s, device_id_type=MESH).wait_recv()

    def send_w(s, h, q, to):
        send(weight.at[s, h, q], weight.at[s, h, q], w_sem.at[s, h, q], to)

    def wait_w(s, h, q):
        arrived(weight.at[s, h, q], w_sem.at[s, h, q])

    def send_d(s, q, to):
        send(downf.at[s, q], downf.at[s, q], d_sem.at[s, q], to)

    def wait_d(s, q):
        arrived(downf.at[s, q], d_sem.at[s, q])

    def dequantize(h, q):
        for r in range(half_blocks):
            b = (h * GROUP + q) * half_blocks + r

            def columns(c, _, b=b, r=r):
                cols = pl.ds(pl.multiple_of(c * 256, 256), 256)
                words = codes[b, :, cols]
                absmax = (scale_ref[pl.ds(b, 1), cols].astype(jnp.float32) + 1.0) / 256.0 * col_ref[:, cols]
                for j in range(4):
                    stage[pl.ds(j, 16, stride=4), :] = levels_of(words, j)[:, :128] * absmax[:, :128]
                    stage[pl.ds(64 + j, 16, stride=4), :] = levels_of(words, j)[:, 128:] * absmax[:, 128:]
                weight[z, h, q, pl.ds(r * 64, 64), pl.ds(pl.multiple_of(c * 256, 128), 128)] = stage[0:64].astype(jnp.bfloat16)
                weight[z, h, q, pl.ds(r * 64, 64), pl.ds(pl.multiple_of(c * 256 + 128, 128), 128)] = stage[64:128].astype(jnp.bfloat16)
                return 0

            lax.fori_loop(0, width // 256, columns, 0)

    def tiles(s, h):
        def one(t, _):
            rows = weight[s, h, pl.ds(2 * t, 2)].reshape(tile, width)
            tt = h * 4 + t
            acc = lax.dot_general(grad[...], rows, NT, preferred_element_type=jnp.float32)
            acc += adapter_scale * jnp.dot(mix[...], downf[s, tt], preferred_element_type=jnp.float32)
            slot = s * GROUP + tt
            outb[slot] = acc.astype(jnp.bfloat16)
            pltpu.make_async_copy(outb.at[slot], out_hbm.at[:, pl.ds(pl.multiple_of(slot * tile, tile), tile)],
                                  out_sem.at[slot]).start()
            return 0

        lax.fori_loop(0, 4, one, 0)

    px, py, ps = p + dx, p + dy, p + ds_
    pd = p + dx + dy
    same_core = (p, px, py, pd)
    events = 2 * (Z - 1)

    def passes_on(s):
        return ((s < z) & (z < Z - 1)) | ((s > z) & (z > 0))

    def pass_on(i):
        if 0 <= i < events:
            s, h = source(i // 2), i % 2
            on = passes_on(s)
            pl.when(on)(lambda: wait_w(s, h, p))
            piece = weight.at[s, h, p]
            to = jnp.where(on, z + jnp.where(s < z, 1, -1), source(0))
            send_if(on, piece, piece, w_sem.at[s, h, p], (d, to))

    def at_end(s):
        return (s == 0) | (s == Z - 1)

    def pass_on_diagonal(i):
        for s in (0, Z - 1):
            away = z if s == 0 else Z - 1 - z
            for h in range(2):
                if not 1 <= i - 1 - h <= Z - 2:
                    continue
                on = away == i - 1 - h
                piece = weight.at[s, h, pd]
                pl.when(on)(lambda s=s, h=h: wait_w(s, h, pd))
                to = jnp.where(on, z + (1 if s == 0 else -1), source(0))
                send_if(on, piece, piece, w_sem.at[s, h, pd], (d, to))

    def event(i):
        return source(i // 2), i % 2

    def first(i):
        s, h = event(i)
        pl.when(jnp.logical_not(passes_on(s)))(lambda: wait_w(s, h, p))
        send_w(s, h, p, at_x)
        send_w(s, h, p, at_y)
        send_w(s, h, p, at_s)

    def second(i):
        s, h = event(i)
        inner = jnp.logical_not(at_end(s))
        wait_w(s, h, px)
        if h == 0:
            piece = weight.at[s, h, px]
            send_if(inner, piece, piece, w_sem.at[s, h, px], at_y)
        send_w(s, h, px, at_s)
        wait_w(s, h, py)
        if h == 1:
            piece = weight.at[s, h, py]
            send_if(inner, piece, piece, w_sem.at[s, h, py], at_x)
        send_w(s, h, py, at_s)

    def third(i):
        s, h = event(i)
        pl.when(jnp.logical_not(at_end(s) & passes_on(s)))(lambda: wait_w(s, h, pd))
        send_w(s, h, pd, at_s)

    def use(i):
        s, h = event(i)
        for q in same_core:
            wait_w(s, h, q + ds_)
        tiles(s, h)

    def service(i):
        if i < 2:
            pass_on(i)
        first(i)
        pass_on(i + 2)
        pass_on_diagonal(i)
        for step, back in ((second, 1), (third, 2), (use, 3)):
            if i >= back:
                step(i - back)

    def own(h):
        def one(j, _):
            m = jnp.where(j == GROUP - 3, GROUP - 1, j + 1)
            dequantize(h, p + lax.rem(m, 2) * ds_ + lax.rem(m // 2, 2) * dx + (m // 4) * dy)
            return 0

        lax.fori_loop(0, GROUP - 2, one, 0)
        tiles(z, h)

    loads[0].wait()
    dequantize(0, p)
    pl.semaphore_wait(barrier, (Z - 1) + (pairs - 1) + 1)
    loads[1].wait()
    for k in range(Z - 1):
        send(upf.at[z], upf.at[z], u_sem.at[z], (d, source(k)))
    for c in down_loads:
        c.wait()
    for k in range(Z - 1):
        send_d(z, p, (d, source(k)))
    for h in range(2):
        piece = weight.at[z, h, p]
        for on, to in ((z < Z - 1, jnp.where(z < Z - 1, z + 1, z - 1)), (z > 0, jnp.where(z > 0, z - 1, z + 1))):
            send_if(on, piece, piece, w_sem.at[z, h, p], (d, to))
        if h == 0:
            dequantize(1, p)
    for h in range(2):
        dequantize(h, pd)
        piece = weight.at[z, h, pd]
        send_if(at_end(z), piece, piece, w_sem.at[z, h, pd], (d, jnp.where(z == 0, z + 1, z - 1)))

    loads[2].wait()
    for k in range(Z - 1):
        arrived(upf.at[source(k)], u_sem.at[source(k)])
    mixed = jnp.zeros(mix.shape, jnp.float32)
    for s in range(Z):
        mixed += lax.dot_general(grad[:, s * up_width:(s + 1) * up_width], upf[s], NT,
                                 preferred_element_type=jnp.float32)
    mix[...] = mixed.astype(jnp.bfloat16)

    def down_first():
        for k in range(Z - 1):
            s = source(k)
            wait_d(s, p)
            for to in (at_x, at_y, at_d, at_s):
                send_d(s, p, to)

    def down_second():
        for k in range(Z - 1):
            s = source(k)
            for q in (px, py, pd):
                wait_d(s, q)
                send_d(s, q, at_s)

    def down_third():
        for k in range(Z - 1):
            for q in same_core:
                wait_d(source(k), q + ds_)

    def gradient_terms():
        loads[3].wait()
        mixed_t = mix[...].astype(jnp.float32).T.astype(jnp.bfloat16)

        def one(t, low):
            s, q = t // GROUP, lax.rem(t, GROUP)
            a = acts[:, pl.ds(pl.multiple_of(t * tile, tile), tile)]
            terms[s, :, pl.ds(pl.multiple_of(q * tile, tile), tile)] = jnp.dot(
                mixed_t, a, preferred_element_type=jnp.float32)
            return low + lax.dot_general(a, downf[s, q], NT, preferred_element_type=jnp.float32)

        low = lax.fori_loop(0, Z * GROUP, one, jnp.zeros(mix.shape, jnp.float32))
        low_t = low.astype(jnp.bfloat16).astype(jnp.float32).T.astype(jnp.bfloat16)
        for s in range(Z):
            terms[s, :, shard:shard + up_width] = jnp.dot(
                low_t, grad[:, s * up_width:(s + 1) * up_width], preferred_element_type=jnp.float32)
        mine, theirs = pl.multiple_of(core * RH, RH), pl.multiple_of((1 - core) * RH, RH)
        for s in range(Z):
            g1s[s] = terms[s, pl.ds(theirs, RH), :].astype(jnp.bfloat16)
        send(g1s, g1r, g1_sem.at[0], at_s)

    def reduce_core():
        arrived(g1r, g1_sem.at[0])
        mine = pl.multiple_of(core * RH, RH)
        for s in range(Z):
            total = terms[s, pl.ds(mine, RH), :] + g1r[s].astype(jnp.float32)
            terms[s, pl.ds(mine, RH), :] = total
            g2s[s] = total.astype(jnp.bfloat16)
        for k in range(Z - 1):
            s = source(k)
            send(g2s.at[s], g2r.at[z], g2_sem.at[z], (d, s))

    def reduce_fsdp():
        mine = pl.multiple_of(core * RH, RH)
        total = terms[z, pl.ds(mine, RH), :]
        for k in range(Z - 1):
            s = source(k)
            arrived(g2r.at[s], g2_sem.at[s])
            total += g2r[s].astype(jnp.float32)
        slot = d // 2
        g3r[slot] = total.astype(jnp.bfloat16)
        for o in others:
            send(g3r.at[slot], g3r.at[slot], g3_sem.at[slot], (o, z))

    def reduce_dp():
        for o in others:
            arrived(g3r.at[o // 2], g3_sem.at[o // 2])
        total = g3r[0].astype(jnp.float32)
        for j in range(1, pairs):
            total += g3r[j].astype(jnp.float32)
        fin[core] = factor * total
        send(fin.at[core], fin.at[core], g4_sem.at[0], at_s)

    def finish():
        arrived(fin.at[1 - core], g4_sem.at[0])
        for c in range(2):
            gdown_ref[c * RH:(c + 1) * RH, :] = fin[c, :, :shard]
            gup_ref[c * RH:(c + 1) * RH, :] = fin[c, :, shard:shard + up_width]

    work = [
        lambda: (down_first(), down_second(), own(0)),
        lambda: (down_third(), gradient_terms()),
        lambda: own(1),
        reduce_core,
        reduce_fsdp,
        reduce_dp,
        finish,
    ]
    for i in range(events):
        service(i)
        if i < len(work):
            work[i]()
    use(events - 3)
    third(events - 2)
    use(events - 2)
    for step in work[events:]:
        step()
    second(events - 1)
    third(events - 1)
    use(events - 1)
    for j, c in enumerate(sends):
        if j in conditions:
            pl.when(conditions[j])(c.wait_send)
        else:
            c.wait_send()

    def drain(t, _):
        pltpu.make_async_copy(outb.at[t], out_hbm.at[:, pl.ds(pl.multiple_of(t * tile, tile), tile)],
                              out_sem.at[t]).wait()
        return 0

    lax.fori_loop(0, Z * GROUP, drain, 0)


def solution(mesh):
    Z, DP = mesh.shape["fsdp"], mesh.shape["dp"]
    bf16, f32 = jnp.bfloat16, jnp.float32

    def local(acts, grad_out, codes, scale_codes, col_scale, down_adapter, up_adapter):
        tokens, D = acts.shape
        O = grad_out.shape[1]
        R, shard = down_adapter.shape
        up_width = up_adapter.shape[1]
        tile = shard // GROUP
        wide = shard + up_width
        RH = R // 2
        factor = adapter_scale * float(tokens * Z * DP) ** (-0.5)
        n_sends = 6 + 4 * (Z - 2) + (Z - 1) * (1 + 1 + 2 * 9 + 4 + 3 + 1) + 1 + (DP // 2 - 1) + 1
        DMA = pltpu.SemaphoreType.DMA
        anywhere, vmem = pl.BlockSpec(memory_space=pl.ANY), pl.BlockSpec(memory_space=pltpu.VMEM)
        return pl.pallas_call(
            functools.partial(kernel, Z, DP, factor),
            out_shape=(
                jax.ShapeDtypeStruct((tokens, D), bf16),
                jax.ShapeDtypeStruct((R, shard), f32),
                jax.ShapeDtypeStruct((R, up_width), f32),
            ),
            in_specs=[anywhere, anywhere, anywhere, vmem, vmem, anywhere, anywhere],
            out_specs=(anywhere, vmem, vmem),
            scratch_shapes=[
                pltpu.VMEM((tokens, D), bf16),
                pltpu.VMEM((tokens, O), bf16),
                pltpu.VMEM(codes.shape, jnp.int32),
                pltpu.VMEM((Z, 2, GROUP, tile // 2, O), bf16),
                pltpu.VMEM((Z, GROUP, R, tile), bf16),
                pltpu.VMEM((Z, R, up_width), bf16),
                pltpu.VMEM((128, 128), f32),
                pltpu.VMEM((Z * GROUP, tokens, tile), bf16),
                pltpu.VMEM((tokens, R), bf16),
                pltpu.VMEM((Z, R, wide), f32),
                pltpu.VMEM((Z, RH, wide), bf16),
                pltpu.VMEM((Z, RH, wide), bf16),
                pltpu.VMEM((Z, RH, wide), bf16),
                pltpu.VMEM((Z, RH, wide), bf16),
                pltpu.VMEM((DP // 2, RH, wide), bf16),
                pltpu.VMEM((2, RH, wide), f32),
                DMA((4,)), DMA((GROUP,)), DMA((Z * GROUP,)), DMA((n_sends,)),
                DMA((Z, 2, GROUP)), DMA((Z, GROUP)), DMA((Z,)),
                DMA((1,)), DMA((Z,)), DMA((DP // 2,)), DMA((1,)),
            ],
            compiler_params=pltpu.CompilerParams(
                collective_id=0, has_side_effects=True, vmem_limit_bytes=60 * 1024 * 1024
            ),
        )(acts, grad_out, codes, scale_codes, col_scale.reshape(1, -1), down_adapter, up_adapter)

    placed = (
        P(("dp", "fsdp"), None),
        P(("dp", "fsdp"), None),
        P("fsdp", None, None),
        P("fsdp", None),
        P(),
        P(None, "fsdp"),
        P(None, "fsdp"),
    )
    return jax.shard_map(
        local,
        mesh=mesh,
        in_specs=placed,
        out_specs=(P(("dp", "fsdp"), None), P(None, "fsdp"), P(None, "fsdp")),
        check_vma=False,
    )
```
